32 devices in a mesh: srv: 8 (over y, x, core), head: 4 (over z).
Axes of the slice: x: 2, y: 2, z: 4, core: 2. Of those that a mesh axis runs over, the one named last changes fastest.
Arguments:
- queries: bfloat16 [2048, 8192], P('srv', 'head'), may hold values from -200 to 200
- key_value_pair: bfloat16 [2, 2048, 1024], P(None, 'srv', 'head'), may hold values from -200 to 200
- lengths: int32 [8], replicated, may hold values from 1 to 1024, 2048 in all
Outputs:
- attended: bfloat16 [2048, 8192], P(('srv', 'head'))
The draws below stay inside these ranges and needn't reach their ends.
All inputs are finite; a program needn't handle non-finite values.
Results may differ from the reference program's by a relative error of at most 0.012.
Values may be sent and summed in bfloat16 or wider, within the bound.
A program may use at most 64 MiB of HBM per device.

```python
import math
import jax
import jax.numpy as jnp
import numpy as np
from jax import lax

HQ = 64
KEY_VALUE_HEADS = 8
HEAD_SIZE = 128
TOK_DEV = 256
NDOC = 8
QUERY_PER_KV = 8
SEQUENCE_TOKENS = 2048
LONGEST = 1024
N_SRV = 8


def activations(key):
    base_key = jax.random.fold_in(key, 7)
    key_sample, value_sample, query_sample = jax.random.split(base_key, 3)
    key_rows = jnp.clip(jax.random.normal(key_sample, (SEQUENCE_TOKENS, KEY_VALUE_HEADS, HEAD_SIZE), jnp.float32), -5.0, 5.0)
    value_rows = jnp.clip(jax.random.normal(value_sample, (SEQUENCE_TOKENS, KEY_VALUE_HEADS, HEAD_SIZE), jnp.float32), -5.0, 5.0)
    query_rows = jnp.clip(jax.random.normal(query_sample, (SEQUENCE_TOKENS, KEY_VALUE_HEADS, QUERY_PER_KV, HEAD_SIZE), jnp.float32), -5.0, 5.0)
    packed_pair = jnp.stack([key_rows.reshape(SEQUENCE_TOKENS, KEY_VALUE_HEADS * HEAD_SIZE), value_rows.reshape(SEQUENCE_TOKENS, KEY_VALUE_HEADS * HEAD_SIZE)], axis=0)
    return (query_rows.reshape(SEQUENCE_TOKENS, HQ * HEAD_SIZE), packed_pair)


def draw_queries(key, part):
    return activations(key)[0].astype(jnp.bfloat16)


def draw_key_value_pair(key, part):
    return activations(key)[1].astype(jnp.bfloat16)


def split_up(number_of, total, most, lean):
    weights = [(1 << 20) // math.isqrt(rank ** lean) + 1 for rank in range(2, number_of + 1)]
    spare, holding = total - most - (number_of - 1), [1] * (number_of - 1)
    while spare > 0:
        candidates = [i for i in range(number_of - 1) if holding[i] < most]
        whole, remaining = sum([weights[i] for i in candidates]), spare
        for i in candidates:
            extra = min(most - holding[i], max(1, remaining * weights[i] // whole), spare)
            holding[i] = holding[i] + extra
            spare = spare - extra
    return np.array([most] + holding)


def uneven(stream_key, count, total, most, skew):
    if count == 2:
        one = jax.random.randint(stream_key, (), max(1, total - most), min(most, total - 1) + 1)
        return jnp.stack([one, total - one])
    tallies = jnp.asarray(split_up(count, total, most, skew), jnp.int32)
    pairs = (count - 1) // 2
    source_of, receiver = tallies[1:1 + 2 * pairs:2], tallies[2:2 + 2 * pairs:2]
    slack = jnp.minimum(source_of - 1, most - receiver)
    moved = jax.random.randint(jax.random.fold_in(stream_key, 1), (pairs,), 0, 1 << 20) % (slack + 1)
    tallies = tallies.at[1:1 + 2 * pairs:2].set(source_of - moved).at[2:2 + 2 * pairs:2].set(receiver + moved)
    return tallies[jax.random.permutation(jax.random.fold_in(stream_key, 2), count)]


def setup_inputs(seed: int = 0) -> dict:
    key_list = jax.random.split(jax.random.key(seed), 4)
    return {
        "queries": draw_queries(jax.random.fold_in(key_list[3], 71), 0),
        "key_value_pair": draw_key_value_pair(jax.random.fold_in(key_list[3], 71), 0),
        "lengths": uneven(key_list[2], NDOC, SEQUENCE_TOKENS, LONGEST, 2).astype(jnp.int32),
    }


def doc_start(doc_lengths, row_ids):
    doc_ends = jnp.cumsum(doc_lengths).astype(jnp.int32)
    passed = doc_ends[None, :] <= row_ids[:, None]
    return jnp.max(jnp.where(passed, doc_ends[None, :], 0), axis=1).astype(jnp.int32)


def apply_rotary(vectors, positions):
    half_width = vectors.shape[-1] // 2
    steps_up = jnp.arange(half_width, dtype=jnp.float32) * (2.0 / vectors.shape[-1])
    inverse = jnp.exp(-steps_up * math.log(500000.0))
    angles = positions[:, None] * inverse[None, :]
    cosine = jnp.cos(angles)[:, None, :]
    sine_table = jnp.sin(angles)[:, None, :]
    low_half = vectors[..., :half_width]
    high_half = vectors[..., half_width:]
    return jnp.concatenate([low_half * cosine - high_half * sine_table, high_half * cosine + low_half * sine_table], axis=-1)


def reference(queries, key_value_pair, lengths):
    score_scale = HEAD_SIZE ** -0.5
    row_ids = jnp.arange(SEQUENCE_TOKENS, dtype=jnp.int32)
    starts = doc_start(lengths, row_ids)
    positions = (row_ids - starts).astype(jnp.float32)
    query_rotated = apply_rotary(queries.reshape(SEQUENCE_TOKENS, HQ, HEAD_SIZE).astype(jnp.float32), positions).astype(jnp.bfloat16)
    key_rotated = apply_rotary(key_value_pair[0].reshape(SEQUENCE_TOKENS, KEY_VALUE_HEADS, HEAD_SIZE).astype(jnp.float32), positions).astype(jnp.bfloat16)
    value_rows = key_value_pair[1].reshape(SEQUENCE_TOKENS, KEY_VALUE_HEADS, HEAD_SIZE)
    query_heads = jnp.transpose(query_rotated.reshape(SEQUENCE_TOKENS, KEY_VALUE_HEADS, QUERY_PER_KV, HEAD_SIZE), (1, 0, 2, 3))
    key_heads = jnp.transpose(key_rotated, (1, 0, 2))
    value_heads = jnp.transpose(value_rows, (1, 0, 2))
    pieces = []
    for owner_index in range(N_SRV):
        row_low = owner_index * TOK_DEV
        row_high = row_low + TOK_DEV
        shard_count = owner_index + 1
        own_rows = row_ids[row_low:row_high]
        own_starts = starts[row_low:row_high]
        key_ids = jnp.arange(row_high, dtype=jnp.int32).reshape(shard_count, TOK_DEV)
        allowed = (key_ids[None] <= own_rows[:, None, None]) & (key_ids[None] >= own_starts[:, None, None])

        def one_head(packed, allowed=allowed, shard_count=shard_count):
            head_query, head_key, head_value = packed
            scores = jnp.einsum('rgd,ckd->grck', head_query.astype(jnp.float32),
                                head_key.reshape(shard_count, TOK_DEV, HEAD_SIZE).astype(jnp.float32)) * score_scale
            masked = jnp.where(allowed[None], scores, -1e30)
            shard_max = jnp.max(masked, axis=3)
            weights = jnp.where(allowed[None], jnp.exp(masked - shard_max[..., None]), 0.0)
            shard_total = jnp.sum(weights, axis=3)
            rounded = lax.optimization_barrier(weights.astype(jnp.bfloat16)).astype(jnp.float32)
            part_value = jnp.einsum('grck,ckd->grcd', rounded,
                                    head_value.reshape(shard_count, TOK_DEV, HEAD_SIZE).astype(jnp.float32))
            top_max = jnp.max(shard_max, axis=2)
            share = jnp.exp(shard_max - top_max[..., None])
            summed = jnp.sum(share[..., None] * part_value, axis=2)
            row_total = jnp.sum(share * shard_total, axis=2)
            return summed / row_total[..., None]

        per_head = lax.map(one_head, (query_heads[:, row_low:row_high], key_heads[:, :row_high], value_heads[:, :row_high]))
        pieces.append(jnp.transpose(per_head, (2, 0, 1, 3)).reshape(TOK_DEV, HQ * HEAD_SIZE))
    return jnp.concatenate(pieces, axis=0).astype(jnp.bfloat16)
```

```python
import functools
import math

import jax
import jax.numpy as jnp
from jax import lax
from jax.experimental import pallas as pl
from jax.experimental.pallas import tpu as pltpu
from jax.sharding import PartitionSpec as P

HEAD = 128
MESH = pl.DeviceIdType.MESH


def kernel(cfg, len_ref, q_ref, kv_ref, out_ref, qraw, qrot, kvbuf, kvin, ksend, table, bias, obuf,
           lsem, qs, qr, kvs, kvr, osend, orecv):
    n_srv, n_head, G, back, tok, kvh, per, R, chunk, ndoc = cfg
    heads = kvh * per
    grp = G * tok
    n_grp = n_srv // G
    T = tok // n_head
    longest = back * grp
    W = longest + R
    width = heads * HEAD
    kw = kvh * HEAD
    nblk = grp // R
    nch = heads // chunk
    per_blk = R // T
    cw = chunk * HEAD
    srv = lax.axis_index("srv")
    z = lax.axis_index("head")
    k = srv // G
    a = srv % G

    bar = pltpu.get_barrier_semaphore()

    def greet(s, h):
        pl.semaphore_signal(bar, inc=1, device_id=(s, h), device_id_type=MESH)

    for i in range(1, n_head):
        for b in range(G):
            greet(k * G + b, (z + i) % n_head)
    for i in range(1, G):
        greet(k * G + (a + i) % G, z)
    for d in range(1, back + 1):
        @pl.when(k + d < n_grp)
        def _():
            for b in range(G):
                greet((k + d) * G + b, z)

        @pl.when(k - d >= 0)
        def _():
            for b in range(G):
                greet((k - d) * G + b, z)

    own_kv = pltpu.make_async_copy(kv_ref, kvin, lsem.at[0])
    own_kv.start()
    my_cols = pl.ds(pl.multiple_of(a * width, HEAD), width)
    own_q = pltpu.make_async_copy(q_ref.at[:, my_cols], qraw.at[a], lsem.at[1])
    own_q.start()

    for d in range(1, back + 1):
        @pl.when(k - d < 0)
        def _():
            kvbuf[:, pl.ds((back - d) * grp, grp), :] = jnp.zeros((2, grp, kw), jnp.bfloat16)

    ends = []
    total = jnp.int32(0)
    for i in range(ndoc):
        total = total + len_ref[i]
        ends.append(total)

    lane = lax.broadcasted_iota(jnp.int32, (tok, HEAD), 1)
    low = lane < HEAD // 2
    step_up = jnp.where(low, lane, lane - HEAD // 2).astype(jnp.float32) * (2.0 / HEAD)
    inverse = jnp.exp(-step_up * math.log(500000.0))

    def starts_of(rows):
        start = jnp.zeros_like(rows)
        for e in ends:
            start = jnp.where(e <= rows, e, start)
        return start

    def make_table(b):
        rows = (k * G + b) * tok + lax.broadcasted_iota(jnp.int32, (tok, HEAD), 0)
        angle = (rows - starts_of(rows)).astype(jnp.float32) * inverse
        sine = jnp.sin(angle)
        table[0] = jnp.cos(angle)
        table[1] = jnp.where(low, -sine, sine)

    def rotate(x):
        x = x.astype(jnp.float32)
        return (x * table[0] + pltpu.roll(x, HEAD // 2, 1) * table[1]).astype(jnp.bfloat16)

    make_table(a)
    own_kv.wait()
    for h in range(G * kvh):
        cols = slice(h * HEAD, (h + 1) * HEAD)
        ksend[:, cols] = rotate(kvin[0, :, cols])

    own_rows = pl.ds(pl.multiple_of(back * grp + a * tok, tok), tok)
    kv_cols = pl.ds(pl.multiple_of(a * kw, HEAD), kw)
    kvbuf[0, own_rows, :] = ksend[:, kv_cols]
    kvbuf[1, own_rows, :] = kvin[1, :, kv_cols]

    count = (n_head - 1) * G + (G - 1)
    for d in range(1, back + 1):
        count = count + G * jnp.where(k + d < n_grp, 1, 0) + G * jnp.where(k - d >= 0, 1, 0)
    pl.semaphore_wait(bar, count)

    def kv_copy(d, i, which):
        b = (a + i) % G
        cols = pl.ds(pl.multiple_of(b * kw, HEAD), kw)
        src = ksend.at[:, cols] if which == 0 else kvin.at[1, :, cols]
        rows = pl.ds(pl.multiple_of((back - d) * grp + a * tok, tok), tok)
        return pltpu.make_async_remote_copy(
            src_ref=src, dst_ref=kvbuf.at[which, rows, :],
            send_sem=kvs.at[d, i, which], recv_sem=kvr.at[d, a, which],
            device_id=((k + d) * G + b, z), device_id_type=MESH)

    def kv_wait(d, b, which):
        rows = pl.ds(pl.multiple_of((back - d) * grp + b * tok, tok), tok)
        ref = kvbuf.at[which, rows, :]
        pltpu.make_async_copy(ref, ref, kvr.at[d, b, which]).wait()

    for d in range(1, back + 1):
        @pl.when(k + d < n_grp)
        def _():
            for i in range(G):
                for which in (1, 0):
                    kv_copy(d, i, which).start()
    q_copies = []
    for i in range(1, G):
        b = (a + i) % G
        for which in (1, 0):
            kv_copy(0, i, which).start()
        cols = pl.ds(pl.multiple_of(b * width, HEAD), width)
        c = pltpu.make_async_remote_copy(
            src_ref=q_ref.at[:, cols], dst_ref=qraw.at[a],
            send_sem=qs.at[i], recv_sem=qr.at[a],
            device_id=(k * G + b, z), device_id_type=MESH)
        c.start()
        q_copies.append(c)

    def rotate_queries(b):
        for h in range(heads):
            qrot[h, pl.ds(pl.multiple_of(b * tok, tok), tok), :] = rotate(
                qraw[b, :, h * HEAD:(h + 1) * HEAD])

    own_q.wait()
    rotate_queries(a)
    for i in range(1, G):
        b = (a + i) % G
        make_table(b)
        pltpu.make_async_copy(qraw.at[b], qraw.at[b], qr.at[b]).wait()
        rotate_queries(b)

    for i in range(1, G):
        for which in range(2):
            kv_wait(0, (a + i) % G, which)
    for d in range(1, back + 1):
        @pl.when(k - d >= 0)
        def _():
            for b in range(G):
                for which in range(2):
                    kv_wait(d, b, which)

    nbm = tok // R
    zpart = z * nbm // n_head
    scale = HEAD ** -0.5 * math.log2(math.e)

    def where_of(s):
        blk = s // nch
        c = s % nch
        b = G - 1 - blk % G
        part = (zpart + 1 + blk // G) % nbm
        return blk, c, b, part

    def out_copy(s, j):
        blk, c, b, part = where_of(s)
        dest = part * per_blk + j
        col = pl.multiple_of(z * (G * width) + a * width + c * cw, HEAD)
        src = obuf.at[s, pl.ds(j * T, T), :]
        dst = out_ref.at[:, pl.ds(col, cw)]
        idx = (z * G + a) * nch + c
        remote = pltpu.make_async_remote_copy(
            src_ref=src, dst_ref=dst, send_sem=osend.at[s * per_blk + j], recv_sem=orecv.at[idx],
            device_id=(k * G + b, dest), device_id_type=MESH)
        local = pltpu.make_async_copy(src, dst, orecv.at[idx])
        mine = jnp.logical_and(b == a, dest == z)
        return mine, remote, local

    def one_step(s, carry):
        blk, c, b, part = where_of(s)
        r0 = pl.multiple_of(b * tok + part * R, R)

        @pl.when(c == 0)
        def _():
            rows = k * grp + r0 + lax.broadcasted_iota(jnp.int32, (R, HEAD), 0)
            start = starts_of(rows)
            for j in range(W // HEAD):
                t = (k - back) * grp + r0 + j * HEAD + lax.broadcasted_iota(jnp.int32, (R, HEAD), 1)
                ok = jnp.logical_and(t >= start, t <= rows)
                bias[:, j * HEAD:(j + 1) * HEAD] = jnp.where(ok, 0.0, -1e30)

        kcol = pl.ds(pl.multiple_of((c * chunk // per) * HEAD, HEAD), HEAD)
        keys = kvbuf[0, pl.ds(r0, W), kcol]
        vals = kvbuf[1, pl.ds(r0, W), kcol]
        vals = jnp.concatenate([vals, jnp.ones_like(vals)], axis=1)
        q = qrot[pl.ds(c * chunk, chunk), pl.ds(r0, R), :].reshape(chunk * R, HEAD)
        sc = lax.dot_general(q, keys, (((1,), (1,)), ((), ())), preferred_element_type=jnp.float32)
        sc = (sc.reshape(chunk, R, W) + bias[...][None]).reshape(chunk * R, W)
        top = jnp.max(sc, axis=1, keepdims=True)
        w = jnp.exp2((sc - top) * scale).astype(jnp.bfloat16)
        acc = lax.dot_general(w, vals, (((1,), (0,)), ((), ())), preferred_element_type=jnp.float32)
        o = (acc[:, :HEAD] / acc[:, HEAD:]).astype(jnp.bfloat16)
        for h in range(chunk):
            obuf[s, :, h * HEAD:(h + 1) * HEAD] = o[h * R:(h + 1) * R, :]

        for j in range(per_blk):
            mine, remote, local = out_copy(s, j)

            @pl.when(mine)
            def _():
                local.start()

            @pl.when(jnp.logical_not(mine))
            def _():
                remote.start()
        return carry

    lax.fori_loop(0, nblk * nch, one_step, 0)

    for i in range(1, G):
        for which in (1, 0):
            kv_copy(0, i, which).wait_send()
    for c in q_copies:
        c.wait_send()
    for d in range(1, back + 1):
        @pl.when(k + d < n_grp)
        def _():
            for i in range(G):
                for which in (1, 0):
                    kv_copy(d, i, which).wait_send()

    def end_send(s, carry):
        for j in range(per_blk):
            mine, remote, local = out_copy(s, j)

            @pl.when(jnp.logical_not(mine))
            def _():
                remote.wait_send()
        return carry

    lax.fori_loop(0, nblk * nch, end_send, 0)

    def end_recv(i, carry):
        col = pl.multiple_of(i * cw, HEAD)
        ref = out_ref.at[:, pl.ds(col, cw)]
        pltpu.make_async_copy(ref, ref, orecv.at[i]).wait()
        return carry

    lax.fori_loop(0, n_head * G * nch, end_recv, 0)


def solution(mesh):
    n_srv, n_head = mesh.shape["srv"], mesh.shape["head"]

    def body(queries, key_value_pair, lengths):
        tok, qw = queries.shape
        kv_all = key_value_pair.shape[2] // HEAD
        G = 2 if kv_all % 2 == 0 and n_srv % 2 == 0 else 1
        kvh = kv_all // G
        per = qw // HEAD // kv_all
        grp = G * tok
        n_grp = n_srv // G
        back = n_grp // 2
        T = tok // n_head
        R = max(tok // 2, T)
        chunk = per // 2
        ndoc = lengths.shape[0]
        heads = kvh * per
        nsteps = (grp // R) * (heads // chunk)
        W = back * grp + R
        cfg = (n_srv, n_head, G, back, tok, kvh, per, R, chunk, ndoc)
        bf = jnp.bfloat16
        dma = pltpu.SemaphoreType.DMA
        return pl.pallas_call(
            functools.partial(kernel, cfg),
            out_shape=jax.ShapeDtypeStruct((T, qw * n_head), bf),
            in_specs=[
                pl.BlockSpec(memory_space=pltpu.SMEM),
                pl.BlockSpec(memory_space=pl.ANY),
                pl.BlockSpec(memory_space=pl.ANY),
            ],
            out_specs=pl.BlockSpec(memory_space=pl.ANY),
            scratch_shapes=[
                pltpu.VMEM((G, tok, heads * HEAD), bf),
                pltpu.VMEM((heads, grp, HEAD), bf),
                pltpu.VMEM((2, (back + 1) * grp, kvh * HEAD), bf),
                pltpu.VMEM((2, tok, kv_all * HEAD), bf),
                pltpu.VMEM((tok, kv_all * HEAD), bf),
                pltpu.VMEM((2, tok, HEAD), jnp.float32),
                pltpu.VMEM((R, W), jnp.float32),
                pltpu.VMEM((nsteps, R, chunk * HEAD), bf),
                dma((2,)),
                dma((G,)),
                dma((G,)),
                dma((back + 1, G, 2)),
                dma((back + 1, G, 2)),
                dma((nsteps * (R // T),)),
                dma((n_head * G * (heads // chunk),)),
            ],
            compiler_params=pltpu.CompilerParams(collective_id=0, has_side_effects=True),
            name="attend",
        )(lengths, queries, key_value_pair)

    in_specs = (P("srv", "head"), P(None, "srv", "head"), P())
    out_specs = P(("srv", "head"), None)
    return jax.shard_map(body, mesh=mesh, in_specs=in_specs, out_specs=out_specs, check_vma=False)
```

```python
import functools
import math

import jax
import jax.numpy as jnp
from jax import lax
from jax.experimental import pallas as pl
from jax.experimental.pallas import tpu as pltpu
from jax.sharding import PartitionSpec as P

HEAD = 128
MESH = pl.DeviceIdType.MESH


def kernel(cfg, len_ref, q_ref, kv_ref, out_ref, qraw, qrot, kvbuf, kvin, ksend, table, bias, obuf,
           lsem, qs, qr, kvs, kvr, fwd, osend, orecv):
    n_srv, n_head, G, back, tok, kvh, per, R, chunk, ndoc = cfg
    heads = kvh * per
    grp = G * tok
    n_grp = n_srv // G
    T = tok // n_head
    longest = back * grp
    W = longest + R
    width = heads * HEAD
    kw = kvh * HEAD
    nblk = grp // R
    nch = heads // chunk
    per_blk = R // T
    cw = chunk * HEAD
    srv = lax.axis_index("srv")
    z = lax.axis_index("head")
    k = srv // G
    a = srv % G

    bar = pltpu.get_barrier_semaphore()

    def greet(s, h):
        pl.semaphore_signal(bar, inc=1, device_id=(s, h), device_id_type=MESH)

    for i in range(1, n_head):
        for b in range(G):
            greet(k * G + b, (z + i) % n_head)
    for i in range(1, G):
        greet(k * G + (a + i) % G, z)
    for d in range(1, back + 1):
        @pl.when(k + d < n_grp)
        def _():
            for b in range(G):
                greet((k + d) * G + b, z)

        @pl.when(k - d >= 0)
        def _():
            for b in range(G):
                greet((k - d) * G + b, z)

    own_kv = pltpu.make_async_copy(kv_ref, kvin, lsem.at[0])
    own_kv.start()
    my_cols = pl.ds(pl.multiple_of(a * width, HEAD), width)
    own_q = pltpu.make_async_copy(q_ref.at[:, my_cols], qraw.at[a], lsem.at[1])
    own_q.start()

    for d in range(1, back + 1):
        @pl.when(k - d < 0)
        def _():
            kvbuf[:, pl.ds((back - d) * grp, grp), :] = jnp.zeros((2, grp, kw), jnp.bfloat16)

    ends = []
    total = jnp.int32(0)
    for i in range(ndoc):
        total = total + len_ref[i]
        ends.append(total)

    lane = lax.broadcasted_iota(jnp.int32, (tok, HEAD), 1)
    low = lane < HEAD // 2
    step_up = jnp.where(low, lane, lane - HEAD // 2).astype(jnp.float32) * (2.0 / HEAD)
    inverse = jnp.exp(-step_up * math.log(500000.0))

    def starts_of(rows):
        start = jnp.zeros_like(rows)
        for e in ends:
            start = jnp.where(e <= rows, e, start)
        return start

    def make_table(b):
        rows = (k * G + b) * tok + lax.broadcasted_iota(jnp.int32, (tok, HEAD), 0)
        angle = (rows - starts_of(rows)).astype(jnp.float32) * inverse
        sine = jnp.sin(angle)
        table[0] = jnp.cos(angle)
        table[1] = jnp.where(low, -sine, sine)

    def rotate(x):
        x = x.astype(jnp.float32)
        return (x * table[0] + pltpu.roll(x, HEAD // 2, 1) * table[1]).astype(jnp.bfloat16)

    make_table(a)
    own_kv.wait()
    for h in range(G * kvh):
        cols = slice(h * HEAD, (h + 1) * HEAD)
        ksend[:, cols] = rotate(kvin[0, :, cols])

    own_rows = pl.ds(pl.multiple_of(back * grp + a * tok, tok), tok)
    kv_cols = pl.ds(pl.multiple_of(a * kw, HEAD), kw)
    kvbuf[0, own_rows, :] = ksend[:, kv_cols]
    kvbuf[1, own_rows, :] = kvin[1, :, kv_cols]

    count = (n_head - 1) * G + (G - 1)
    for d in range(1, back + 1):
        count = count + G * jnp.where(k + d < n_grp, 1, 0) + G * jnp.where(k - d >= 0, 1, 0)
    pl.semaphore_wait(bar, count)

    def kv_copy(d, i, which):
        b = (a + i) % G
        cols = pl.ds(pl.multiple_of(b * kw, HEAD), kw)
        src = ksend.at[:, cols] if which == 0 else kvin.at[1, :, cols]
        rows = pl.ds(pl.multiple_of((back - d) * grp + a * tok, tok), tok)
        return pltpu.make_async_remote_copy(
            src_ref=src, dst_ref=kvbuf.at[which, rows, :],
            send_sem=kvs.at[d, i, which], recv_sem=kvr.at[d, a, which],
            device_id=((k + d) * G + b, z), device_id_type=MESH)

    def kv_wait(d, b, which):
        rows = pl.ds(pl.multiple_of((back - d) * grp + b * tok, tok), tok)
        ref = kvbuf.at[which, rows, :]
        pltpu.make_async_copy(ref, ref, kvr.at[d, b, which]).wait()

    relayed = jnp.logical_and(k % 2 == 1, k + 2 < n_grp)
    relays = jnp.logical_and(k % 2 == 1, k >= 3)

    def sends(d):
        near = k + d < n_grp
        if d == 1 and back >= 2:
            near = jnp.logical_and(near, jnp.logical_not(relayed))
        return near

    def relay_copy(b, which):
        src = pl.ds(pl.multiple_of((back - 2) * grp + b * tok, tok), tok)
        dst = pl.ds(pl.multiple_of((back - 1) * grp + b * tok, tok), tok)
        return pltpu.make_async_remote_copy(
            src_ref=kvbuf.at[which, src, :], dst_ref=kvbuf.at[which, dst, :],
            send_sem=fwd.at[b, which], recv_sem=kvr.at[1, b, which],
            device_id=(srv - G, z), device_id_type=MESH)

    for d in range(1, back + 1):
        @pl.when(sends(d))
        def _():
            for i in range(G):
                for which in (1, 0):
                    kv_copy(d, i, which).start()
    q_copies = []
    for i in range(1, G):
        b = (a + i) % G
        for which in (1, 0):
            kv_copy(0, i, which).start()
        cols = pl.ds(pl.multiple_of(b * width, HEAD), width)
        c = pltpu.make_async_remote_copy(
            src_ref=q_ref.at[:, cols], dst_ref=qraw.at[a],
            send_sem=qs.at[i], recv_sem=qr.at[a],
            device_id=(k * G + b, z), device_id_type=MESH)
        c.start()
        q_copies.append(c)

    def rotate_queries(b):
        for h in range(heads):
            qrot[h, pl.ds(pl.multiple_of(b * tok, tok), tok), :] = rotate(
                qraw[b, :, h * HEAD:(h + 1) * HEAD])

    own_q.wait()
    rotate_queries(a)
    for i in range(1, G):
        b = (a + i) % G
        make_table(b)
        pltpu.make_async_copy(qraw.at[b], qraw.at[b], qr.at[b]).wait()
        rotate_queries(b)

    for i in range(1, G):
        for which in range(2):
            kv_wait(0, (a + i) % G, which)
    order = [2, 1] + list(range(3, back + 1)) if back >= 2 else [1]
    for d in order:
        @pl.when(k - d >= 0)
        def _():
            for b in range(G):
                for which in (1, 0):
                    kv_wait(d, b, which)
                    if d == 2:
                        @pl.when(relays)
                        def _():
                            relay_copy(b, which).start()

    nbm = tok // R
    zpart = z * nbm // n_head
    edge = n_head // 4
    outer = jnp.logical_or(z < edge, z >= n_head - edge)
    scale = HEAD ** -0.5 * math.log2(math.e)

    def where_of(s):
        blk = s // nch
        c = s % nch
        late = jnp.where(blk == 0, 0, jnp.where(blk == nblk - 1, 1, blk + 1))
        blk = jnp.where(outer, late, blk)
        b = G - 1 - blk % G
        part = (zpart + 1 + blk // G) % nbm
        return blk, c, b, part

    def out_copy(s, j):
        blk, c, b, part = where_of(s)
        dest = part * per_blk + j
        col = pl.multiple_of(z * (G * width) + a * width + c * cw, HEAD)
        src = obuf.at[s, pl.ds(j * T, T), :]
        dst = out_ref.at[:, pl.ds(col, cw)]
        idx = (z * G + a) * nch + c
        remote = pltpu.make_async_remote_copy(
            src_ref=src, dst_ref=dst, send_sem=osend.at[s * per_blk + j], recv_sem=orecv.at[idx],
            device_id=(k * G + b, dest), device_id_type=MESH)
        local = pltpu.make_async_copy(src, dst, orecv.at[idx])
        mine = jnp.logical_and(b == a, dest == z)
        return mine, remote, local

    def one_step(s, carry):
        blk, c, b, part = where_of(s)
        r0 = pl.multiple_of(b * tok + part * R, R)

        @pl.when(c == 0)
        def _():
            rows = k * grp + r0 + lax.broadcasted_iota(jnp.int32, (R, HEAD), 0)
            start = starts_of(rows)
            for j in range(W // HEAD):
                t = (k - back) * grp + r0 + j * HEAD + lax.broadcasted_iota(jnp.int32, (R, HEAD), 1)
                ok = jnp.logical_and(t >= start, t <= rows)
                bias[:, j * HEAD:(j + 1) * HEAD] = jnp.where(ok, 0.0, -1e30)

        kcol = pl.ds(pl.multiple_of((c * chunk // per) * HEAD, HEAD), HEAD)
        keys = kvbuf[0, pl.ds(r0, W), kcol]
        vals = kvbuf[1, pl.ds(r0, W), kcol]
        vals = jnp.concatenate([vals, jnp.ones_like(vals)], axis=1)
        q = qrot[pl.ds(c * chunk, chunk), pl.ds(r0, R), :].reshape(chunk * R, HEAD)
        sc = lax.dot_general(q, keys, (((1,), (1,)), ((), ())), preferred_element_type=jnp.float32)
        sc = (sc.reshape(chunk, R, W) + bias[...][None]).reshape(chunk * R, W)
        top = jnp.max(sc, axis=1, keepdims=True)
        w = jnp.exp2((sc - top) * scale).astype(jnp.bfloat16)
        acc = lax.dot_general(w, vals, (((1,), (0,)), ((), ())), preferred_element_type=jnp.float32)
        o = (acc[:, :HEAD] / acc[:, HEAD:]).astype(jnp.bfloat16)
        for h in range(chunk):
            obuf[s, :, h * HEAD:(h + 1) * HEAD] = o[h * R:(h + 1) * R, :]

        for j in range(per_blk):
            mine, remote, local = out_copy(s, j)

            @pl.when(mine)
            def _():
                local.start()

            @pl.when(jnp.logical_not(mine))
            def _():
                remote.start()
        return carry

    lax.fori_loop(0, nblk * nch, one_step, 0)

    for i in range(1, G):
        for which in (1, 0):
            kv_copy(0, i, which).wait_send()
    for c in q_copies:
        c.wait_send()
    for d in range(1, back + 1):
        @pl.when(sends(d))
        def _():
            for i in range(G):
                for which in (1, 0):
                    kv_copy(d, i, which).wait_send()
    if back >= 2:
        @pl.when(relays)
        def _():
            for b in range(G):
                for which in (1, 0):
                    relay_copy(b, which).wait_send()

    def end_send(s, carry):
        for j in range(per_blk):
            mine, remote, local = out_copy(s, j)

            @pl.when(jnp.logical_not(mine))
            def _():
                remote.wait_send()
        return carry

    lax.fori_loop(0, nblk * nch, end_send, 0)

    def end_recv(i, carry):
        col = pl.multiple_of(i * cw, HEAD)
        ref = out_ref.at[:, pl.ds(col, cw)]
        pltpu.make_async_copy(ref, ref, orecv.at[i]).wait()
        return carry

    lax.fori_loop(0, n_head * G * nch, end_recv, 0)


def solution(mesh):
    n_srv, n_head = mesh.shape["srv"], mesh.shape["head"]

    def body(queries, key_value_pair, lengths):
        tok, qw = queries.shape
        kv_all = key_value_pair.shape[2] // HEAD
        G = 2 if kv_all % 2 == 0 and n_srv % 2 == 0 else 1
        kvh = kv_all // G
        per = qw // HEAD // kv_all
        grp = G * tok
        n_grp = n_srv // G
        back = n_grp // 2
        T = tok // n_head
        R = max(tok // 2, T)
        chunk = per // 2
        ndoc = lengths.shape[0]
        heads = kvh * per
        nsteps = (grp // R) * (heads // chunk)
        W = back * grp + R
        cfg = (n_srv, n_head, G, back, tok, kvh, per, R, chunk, ndoc)
        bf = jnp.bfloat16
        dma = pltpu.SemaphoreType.DMA
        return pl.pallas_call(
            functools.partial(kernel, cfg),
            out_shape=jax.ShapeDtypeStruct((T, qw * n_head), bf),
            in_specs=[
                pl.BlockSpec(memory_space=pltpu.SMEM),
                pl.BlockSpec(memory_space=pl.ANY),
                pl.BlockSpec(memory_space=pl.ANY),
            ],
            out_specs=pl.BlockSpec(memory_space=pl.ANY),
            scratch_shapes=[
                pltpu.VMEM((G, tok, heads * HEAD), bf),
                pltpu.VMEM((heads, grp, HEAD), bf),
                pltpu.VMEM((2, (back + 1) * grp, kvh * HEAD), bf),
                pltpu.VMEM((2, tok, kv_all * HEAD), bf),
                pltpu.VMEM((tok, kv_all * HEAD), bf),
                pltpu.VMEM((2, tok, HEAD), jnp.float32),
                pltpu.VMEM((R, W), jnp.float32),
                pltpu.VMEM((nsteps, R, chunk * HEAD), bf),
                dma((2,)),
                dma((G,)),
                dma((G,)),
                dma((back + 1, G, 2)),
                dma((back + 1, G, 2)),
                dma((G, 2)),
                dma((nsteps * (R // T),)),
                dma((n_head * G * (heads // chunk),)),
            ],
            compiler_params=pltpu.CompilerParams(collective_id=0, has_side_effects=True),
            name="attend",
        )(lengths, queries, key_value_pair)

    in_specs = (P("srv", "head"), P(None, "srv", "head"), P())
    out_specs = P(("srv", "head"), None)
    return jax.shard_map(body, mesh=mesh, in_specs=in_specs, out_specs=out_specs, check_vma=False)
```

```python
import functools
import math

import jax
import jax.numpy as jnp
from jax import lax
from jax.experimental import pallas as pl
from jax.experimental.pallas import tpu as pltpu
from jax.sharding import PartitionSpec as P

HEAD = 128
MESH = pl.DeviceIdType.MESH


def kernel(cfg, len_ref, q_ref, kv_ref, out_ref, qraw, qrot, kvbuf, kvin, ksend, table, bias, obuf,
           lsem, qs, qr, kvs, kvr, fwd, osend, orecv):
    n_srv, n_head, G, back, tok, kvh, per, R, chunk, ndoc = cfg
    heads = kvh * per
    grp = G * tok
    n_grp = n_srv // G
    T = tok // n_head
    longest = back * grp
    W = longest + R
    width = heads * HEAD
    kw = kvh * HEAD
    nblk = grp // R
    nch = heads // chunk
    per_blk = R // T
    cw = chunk * HEAD
    srv = lax.axis_index("srv")
    z = lax.axis_index("head")
    k = srv // G
    a = srv % G

    bar = pltpu.get_barrier_semaphore()

    def greet(s, h):
        pl.semaphore_signal(bar, inc=1, device_id=(s, h), device_id_type=MESH)

    for i in range(1, n_head):
        for b in range(G):
            greet(k * G + b, (z + i) % n_head)
    for i in range(1, G):
        greet(k * G + (a + i) % G, z)
    for d in range(1, back + 1):
        @pl.when(k + d < n_grp)
        def _():
            for b in range(G):
                greet((k + d) * G + b, z)

        @pl.when(k - d >= 0)
        def _():
            for b in range(G):
                greet((k - d) * G + b, z)

    own_kv = pltpu.make_async_copy(kv_ref, kvin, lsem.at[0])
    own_kv.start()
    my_cols = pl.ds(pl.multiple_of(a * width, HEAD), width)
    own_q = pltpu.make_async_copy(q_ref.at[:, my_cols], qraw.at[a], lsem.at[1])
    own_q.start()

    for d in range(1, back + 1):
        @pl.when(k - d < 0)
        def _():
            kvbuf[:, pl.ds((back - d) * grp, grp), :] = jnp.zeros((2, grp, kw), jnp.bfloat16)

    ends = []
    total = jnp.int32(0)
    for i in range(ndoc):
        total = total + len_ref[i]
        ends.append(total)

    lane = lax.broadcasted_iota(jnp.int32, (tok, HEAD), 1)
    low = lane < HEAD // 2
    step_up = jnp.where(low, lane, lane - HEAD // 2).astype(jnp.float32) * (2.0 / HEAD)
    inverse = jnp.exp(-step_up * math.log(500000.0))

    def starts_of(rows):
        start = jnp.zeros_like(rows)
        for e in ends:
            start = jnp.where(e <= rows, e, start)
        return start

    def make_table(b):
        rows = (k * G + b) * tok + lax.broadcasted_iota(jnp.int32, (tok, HEAD), 0)
        angle = (rows - starts_of(rows)).astype(jnp.float32) * inverse
        sine = jnp.sin(angle)
        table[0] = jnp.cos(angle)
        table[1] = jnp.where(low, -sine, sine)

    def rotate(x):
        x = x.astype(jnp.float32)
        return (x * table[0] + pltpu.roll(x, HEAD // 2, 1) * table[1]).astype(jnp.bfloat16)

    make_table(a)
    own_kv.wait()
    for h in range(G * kvh):
        cols = slice(h * HEAD, (h + 1) * HEAD)
        ksend[:, cols] = rotate(kvin[0, :, cols])

    own_rows = pl.ds(pl.multiple_of(back * grp + a * tok, tok), tok)
    kv_cols = pl.ds(pl.multiple_of(a * kw, HEAD), kw)
    kvbuf[0, own_rows, :] = ksend[:, kv_cols]
    kvbuf[1, own_rows, :] = kvin[1, :, kv_cols]

    count = (n_head - 1) * G + (G - 1)
    for d in range(1, back + 1):
        count = count + G * jnp.where(k + d < n_grp, 1, 0) + G * jnp.where(k - d >= 0, 1, 0)
    pl.semaphore_wait(bar, count)

    def kv_copy(d, i, which):
        b = (a + i) % G
        cols = pl.ds(pl.multiple_of(b * kw, HEAD), kw)
        src = ksend.at[:, cols] if which == 0 else kvin.at[1, :, cols]
        rows = pl.ds(pl.multiple_of((back - d) * grp + a * tok, tok), tok)
        return pltpu.make_async_remote_copy(
            src_ref=src, dst_ref=kvbuf.at[which, rows, :],
            send_sem=kvs.at[d, i, which], recv_sem=kvr.at[d, a, which],
            device_id=((k + d) * G + b, z), device_id_type=MESH)

    def kv_wait(d, b, which):
        rows = pl.ds(pl.multiple_of((back - d) * grp + b * tok, tok), tok)
        ref = kvbuf.at[which, rows, :]
        pltpu.make_async_copy(ref, ref, kvr.at[d, b, which]).wait()

    relayed = jnp.logical_and(jnp.logical_and(k % 2 == 1, k + 2 < n_grp), a == G - 1)
    relays = jnp.logical_and(k % 2 == 1, k >= 3)

    def sends(d):
        near = k + d < n_grp
        if d == 1 and back >= 2:
            near = jnp.logical_and(near, jnp.logical_not(relayed))
        return near

    def relay_copy(b, which):
        src = pl.ds(pl.multiple_of((back - 2) * grp + b * tok, tok), tok)
        dst = pl.ds(pl.multiple_of((back - 1) * grp + b * tok, tok), tok)
        return pltpu.make_async_remote_copy(
            src_ref=kvbuf.at[which, src, :], dst_ref=kvbuf.at[which, dst, :],
            send_sem=fwd.at[b, which], recv_sem=kvr.at[1, b, which],
            device_id=(srv - G, z), device_id_type=MESH)

    def start_kv(d, when):
        @pl.when(jnp.logical_and(sends(d), when))
        def _():
            for i in range(G):
                for which in range(2):
                    kv_copy(d, i, which).start()

    for d in range(1, back + 1):
        start_kv(d, a == G - 1 if d == back else True)
    q_copies = []
    for i in range(1, G):
        b = (a + i) % G
        for which in range(2):
            kv_copy(0, i, which).start()
        cols = pl.ds(pl.multiple_of(b * width, HEAD), width)
        c = pltpu.make_async_remote_copy(
            src_ref=q_ref.at[:, cols], dst_ref=qraw.at[a],
            send_sem=qs.at[i], recv_sem=qr.at[a],
            device_id=(k * G + b, z), device_id_type=MESH)
        c.start()
        q_copies.append(c)

    def rotate_queries(b):
        for h in range(heads):
            qrot[h, pl.ds(pl.multiple_of(b * tok, tok), tok), :] = rotate(
                qraw[b, :, h * HEAD:(h + 1) * HEAD])

    own_q.wait()
    rotate_queries(a)
    start_kv(back, a < G - 1)
    for i in range(1, G):
        b = (a + i) % G
        make_table(b)
        pltpu.make_async_copy(qraw.at[b], qraw.at[b], qr.at[b]).wait()
        rotate_queries(b)

    if back >= 2:
        @pl.when(k >= 2)
        def _():
            for which in range(2):
                kv_wait(2, G - 1, which)

                @pl.when(relays)
                def _():
                    relay_copy(G - 1, which).start()

    def wait_early(which):
        for i in range(1, G):
            kv_wait(0, (a + i) % G, which)
        for d in range(1, back + 1):
            @pl.when(k - d >= 0)
            def _():
                for b in range(G - 1 if d == back else 0, G):
                    if (d, b) != (2, G - 1):
                        kv_wait(d, b, which)

    def wait_late():
        @pl.when(k - back >= 0)
        def _():
            for b in range(G - 1):
                for which in range(2):
                    kv_wait(back, b, which)

    wait_early(0)

    nbm = tok // R
    zpart = z * nbm // n_head
    edge = n_head // 4
    outer = jnp.logical_or(z < edge, z >= n_head - edge)
    scale = HEAD ** -0.5 * math.log2(math.e)

    def where_of(s):
        blk = s // nch
        c = s % nch
        late = jnp.where(blk == 0, 0, jnp.where(blk == nblk - 1, 1, blk + 1))
        blk = jnp.where(outer, late, blk)
        b = G - 1 - blk % G
        part = (zpart + 1 + blk // G) % nbm
        return blk, c, b, part

    def out_copy(s, j):
        blk, c, b, part = where_of(s)
        dest = part * per_blk + j
        col = pl.multiple_of(z * (G * width) + a * width + c * cw, HEAD)
        src = obuf.at[s, pl.ds(j * T, T), :]
        dst = out_ref.at[:, pl.ds(col, cw)]
        idx = (z * G + a) * nch + c
        remote = pltpu.make_async_remote_copy(
            src_ref=src, dst_ref=dst, send_sem=osend.at[s * per_blk + j], recv_sem=orecv.at[idx],
            device_id=(k * G + b, dest), device_id_type=MESH)
        local = pltpu.make_async_copy(src, dst, orecv.at[idx])
        mine = jnp.logical_and(b == a, dest == z)
        return mine, remote, local

    def one_step(s, carry):
        blk, c, b, part = where_of(s)
        r0 = pl.multiple_of(b * tok + part * R, R)

        @pl.when(s == nch)
        def _():
            wait_late()

        @pl.when(c == 0)
        def _():
            rows = k * grp + r0 + lax.broadcasted_iota(jnp.int32, (R, HEAD), 0)
            start = starts_of(rows)
            for j in range(W // HEAD):
                t = (k - back) * grp + r0 + j * HEAD + lax.broadcasted_iota(jnp.int32, (R, HEAD), 1)
                ok = jnp.logical_and(t >= start, t <= rows)
                bias[:, j * HEAD:(j + 1) * HEAD] = jnp.where(ok, 0.0, -1e30)

        kcol = pl.ds(pl.multiple_of((c * chunk // per) * HEAD, HEAD), HEAD)
        keys = kvbuf[0, pl.ds(r0, W), kcol]
        q = qrot[pl.ds(c * chunk, chunk), pl.ds(r0, R), :].reshape(chunk * R, HEAD)
        sc = lax.dot_general(q, keys, (((1,), (1,)), ((), ())), preferred_element_type=jnp.float32)
        sc = (sc.reshape(chunk, R, W) + bias[...][None]).reshape(chunk * R, W)
        top = jnp.max(sc, axis=1, keepdims=True)
        w = jnp.exp2((sc - top) * scale).astype(jnp.bfloat16)

        @pl.when(s == 0)
        def _():
            wait_early(1)

        vals = kvbuf[1, pl.ds(r0, W), kcol]
        vals = jnp.concatenate([vals, jnp.ones_like(vals)], axis=1)
        acc = lax.dot_general(w, vals, (((1,), (0,)), ((), ())), preferred_element_type=jnp.float32)
        o = (acc[:, :HEAD] / acc[:, HEAD:]).astype(jnp.bfloat16)
        for h in range(chunk):
            obuf[s, :, h * HEAD:(h + 1) * HEAD] = o[h * R:(h + 1) * R, :]

        for j in range(per_blk):
            mine, remote, local = out_copy(s, j)

            @pl.when(mine)
            def _():
                local.start()

            @pl.when(jnp.logical_not(mine))
            def _():
                remote.start()
        return carry

    lax.fori_loop(0, nblk * nch, one_step, 0)

    for i in range(1, G):
        for which in (1, 0):
            kv_copy(0, i, which).wait_send()
    for c in q_copies:
        c.wait_send()
    for d in range(1, back + 1):
        @pl.when(sends(d))
        def _():
            for i in range(G):
                for which in (1, 0):
                    kv_copy(d, i, which).wait_send()
    if back >= 2:
        @pl.when(relays)
        def _():
            for which in range(2):
                relay_copy(G - 1, which).wait_send()

    def end_send(s, carry):
        for j in range(per_blk):
            mine, remote, local = out_copy(s, j)

            @pl.when(jnp.logical_not(mine))
            def _():
                remote.wait_send()
        return carry

    lax.fori_loop(0, nblk * nch, end_send, 0)

    def end_recv(i, carry):
        col = pl.multiple_of(i * cw, HEAD)
        ref = out_ref.at[:, pl.ds(col, cw)]
        pltpu.make_async_copy(ref, ref, orecv.at[i]).wait()
        return carry

    lax.fori_loop(0, n_head * G * nch, end_recv, 0)


def solution(mesh):
    n_srv, n_head = mesh.shape["srv"], mesh.shape["head"]

    def body(queries, key_value_pair, lengths):
        tok, qw = queries.shape
        kv_all = key_value_pair.shape[2] // HEAD
        G = 2 if kv_all % 2 == 0 and n_srv % 2 == 0 else 1
        kvh = kv_all // G
        per = qw // HEAD // kv_all
        grp = G * tok
        n_grp = n_srv // G
        back = n_grp // 2
        T = tok // n_head
        R = max(tok // 2, T)
        chunk = per // 2
        ndoc = lengths.shape[0]
        heads = kvh * per
        nsteps = (grp // R) * (heads // chunk)
        W = back * grp + R
        cfg = (n_srv, n_head, G, back, tok, kvh, per, R, chunk, ndoc)
        bf = jnp.bfloat16
        dma = pltpu.SemaphoreType.DMA
        return pl.pallas_call(
            functools.partial(kernel, cfg),
            out_shape=jax.ShapeDtypeStruct((T, qw * n_head), bf),
            in_specs=[
                pl.BlockSpec(memory_space=pltpu.SMEM),
                pl.BlockSpec(memory_space=pl.ANY),
                pl.BlockSpec(memory_space=pl.ANY),
            ],
            out_specs=pl.BlockSpec(memory_space=pl.ANY),
            scratch_shapes=[
                pltpu.VMEM((G, tok, heads * HEAD), bf),
                pltpu.VMEM((heads, grp, HEAD), bf),
                pltpu.VMEM((2, (back + 1) * grp, kvh * HEAD), bf),
                pltpu.VMEM((2, tok, kv_all * HEAD), bf),
                pltpu.VMEM((tok, kv_all * HEAD), bf),
                pltpu.VMEM((2, tok, HEAD), jnp.float32),
                pltpu.VMEM((R, W), jnp.float32),
                pltpu.VMEM((nsteps, R, chunk * HEAD), bf),
                dma((2,)),
                dma((G,)),
                dma((G,)),
                dma((back + 1, G, 2)),
                dma((back + 1, G, 2)),
                dma((G, 2)),
                dma((nsteps * (R // T),)),
                dma((n_head * G * (heads // chunk),)),
            ],
            compiler_params=pltpu.CompilerParams(collective_id=0, has_side_effects=True),
            name="attend",
        )(lengths, queries, key_value_pair)

    in_specs = (P("srv", "head"), P(None, "srv", "head"), P())
    out_specs = P(("srv", "head"), None)
    return jax.shard_map(body, mesh=mesh, in_specs=in_specs, out_specs=out_specs, check_vma=False)
```

```python
import functools
import math

import jax
import jax.numpy as jnp
from jax import lax
from jax.experimental import pallas as pl
from jax.experimental.pallas import tpu as pltpu
from jax.sharding import PartitionSpec as P

HEAD = 128
MESH = pl.DeviceIdType.MESH


def kernel(cfg, len_ref, q_ref, kv_ref, out_ref, qraw, qrot, kvbuf, kvin, ksend, table, bias, obuf,
           lsem, qs, qr, kvs, kvr, fwd, osend, orecv):
    n_srv, n_head, G, back, tok, kvh, per, R, chunk, ndoc = cfg
    heads = kvh * per
    grp = G * tok
    n_grp = n_srv // G
    T = tok // n_head
    longest = back * grp
    W = longest + R
    width = heads * HEAD
    kw = kvh * HEAD
    nblk = grp // R
    nch = heads // chunk
    per_blk = R // T
    cw = chunk * HEAD
    srv = lax.axis_index("srv")
    z = lax.axis_index("head")
    k = srv // G
    a = srv % G

    bar = pltpu.get_barrier_semaphore()

    def greet(s, h):
        pl.semaphore_signal(bar, inc=1, device_id=(s, h), device_id_type=MESH)

    for i in range(1, n_head):
        for b in range(G):
            greet(k * G + b, (z + i) % n_head)
    for i in range(1, G):
        greet(k * G + (a + i) % G, z)
    for d in range(1, back + 1):
        @pl.when(k + d < n_grp)
        def _():
            for b in range(G):
                greet((k + d) * G + b, z)

        @pl.when(k - d >= 0)
        def _():
            for b in range(G):
                greet((k - d) * G + b, z)

    own_kv = pltpu.make_async_copy(kv_ref, kvin, lsem.at[0])
    own_kv.start()
    my_cols = pl.ds(pl.multiple_of(a * width, HEAD), width)
    own_q = pltpu.make_async_copy(q_ref.at[:, my_cols], qraw.at[a], lsem.at[1])
    own_q.start()

    for d in range(1, back + 1):
        @pl.when(k - d < 0)
        def _():
            kvbuf[:, pl.ds((back - d) * grp, grp), :] = jnp.zeros((2, grp, kw), jnp.bfloat16)

    ends = []
    total = jnp.int32(0)
    for i in range(ndoc):
        total = total + len_ref[i]
        ends.append(total)

    lane = lax.broadcasted_iota(jnp.int32, (tok, HEAD), 1)
    low = lane < HEAD // 2
    step_up = jnp.where(low, lane, lane - HEAD // 2).astype(jnp.float32) * (2.0 / HEAD)
    inverse = jnp.exp(-step_up * math.log(500000.0))

    def starts_of(rows):
        start = jnp.zeros_like(rows)
        for e in ends:
            start = jnp.where(e <= rows, e, start)
        return start

    def make_table(b):
        rows = (k * G + b) * tok + lax.broadcasted_iota(jnp.int32, (tok, HEAD), 0)
        angle = (rows - starts_of(rows)).astype(jnp.float32) * inverse
        sine = jnp.sin(angle)
        table[0] = jnp.cos(angle)
        table[1] = jnp.where(low, -sine, sine)

    def rotate(x):
        x = x.astype(jnp.float32)
        return (x * table[0] + pltpu.roll(x, HEAD // 2, 1) * table[1]).astype(jnp.bfloat16)

    make_table(a)
    own_kv.wait()
    for h in range(G * kvh):
        cols = slice(h * HEAD, (h + 1) * HEAD)
        ksend[:, cols] = rotate(kvin[0, :, cols])

    own_rows = pl.ds(pl.multiple_of(back * grp + a * tok, tok), tok)
    kv_cols = pl.ds(pl.multiple_of(a * kw, HEAD), kw)
    kvbuf[0, own_rows, :] = ksend[:, kv_cols]
    kvbuf[1, own_rows, :] = kvin[1, :, kv_cols]

    count = (n_head - 1) * G + (G - 1)
    for d in range(1, back + 1):
        count = count + G * jnp.where(k + d < n_grp, 1, 0) + G * jnp.where(k - d >= 0, 1, 0)
    pl.semaphore_wait(bar, count)

    def kv_copy(d, i, which):
        b = (a + i) % G
        cols = pl.ds(pl.multiple_of(b * kw, HEAD), kw)
        src = ksend.at[:, cols] if which == 0 else kvin.at[1, :, cols]
        rows = pl.ds(pl.multiple_of((back - d) * grp + a * tok, tok), tok)
        return pltpu.make_async_remote_copy(
            src_ref=src, dst_ref=kvbuf.at[which, rows, :],
            send_sem=kvs.at[d, i, which], recv_sem=kvr.at[d, a, which],
            device_id=((k + d) * G + b, z), device_id_type=MESH)

    def kv_wait(d, b, which):
        rows = pl.ds(pl.multiple_of((back - d) * grp + b * tok, tok), tok)
        ref = kvbuf.at[which, rows, :]
        pltpu.make_async_copy(ref, ref, kvr.at[d, b, which]).wait()

    relayed = jnp.logical_and(jnp.logical_and(k % 2 == 1, k + 2 < n_grp), a == G - 1)
    relays = jnp.logical_and(k % 2 == 1, k >= 3)

    def sends(d):
        near = k + d < n_grp
        if d == 1 and back >= 2:
            near = jnp.logical_and(near, jnp.logical_not(relayed))
        return near

    def relay_copy(b, which):
        src = pl.ds(pl.multiple_of((back - 2) * grp + b * tok, tok), tok)
        dst = pl.ds(pl.multiple_of((back - 1) * grp + b * tok, tok), tok)
        return pltpu.make_async_remote_copy(
            src_ref=kvbuf.at[which, src, :], dst_ref=kvbuf.at[which, dst, :],
            send_sem=fwd.at[b, which], recv_sem=kvr.at[1, b, which],
            device_id=(srv - G, z), device_id_type=MESH)

    def start_kv(d, when):
        @pl.when(jnp.logical_and(sends(d), when))
        def _():
            for i in range(G):
                for which in range(2):
                    kv_copy(d, i, which).start()

    for d in range(1, back + 1):
        start_kv(d, a == G - 1 if d == back else True)
    q_copies = []
    for i in range(1, G):
        b = (a + i) % G
        for which in range(2):
            kv_copy(0, i, which).start()
        cols = pl.ds(pl.multiple_of(b * width, HEAD), width)
        c = pltpu.make_async_remote_copy(
            src_ref=q_ref.at[:, cols], dst_ref=qraw.at[a],
            send_sem=qs.at[i], recv_sem=qr.at[a],
            device_id=(k * G + b, z), device_id_type=MESH)
        c.start()
        q_copies.append(c)

    def rotate_queries(b):
        for h in range(heads):
            qrot[h, pl.ds(pl.multiple_of(b * tok, tok), tok), :] = rotate(
                qraw[b, :, h * HEAD:(h + 1) * HEAD])

    own_q.wait()
    rotate_queries(a)
    start_kv(back, a < G - 1)
    for i in range(1, G):
        b = (a + i) % G
        make_table(b)
        pltpu.make_async_copy(qraw.at[b], qraw.at[b], qr.at[b]).wait()
        rotate_queries(b)

    if back >= 2:
        @pl.when(k >= 2)
        def _():
            for which in range(2):
                kv_wait(2, G - 1, which)

                @pl.when(relays)
                def _():
                    relay_copy(G - 1, which).start()

    def wait_early(which):
        for i in range(1, G):
            kv_wait(0, (a + i) % G, which)
        for d in range(1, back + 1):
            @pl.when(k - d >= 0)
            def _():
                for b in range(G - 1 if d == back else 0, G):
                    if (d, b) != (2, G - 1):
                        kv_wait(d, b, which)

    def wait_late():
        @pl.when(k - back >= 0)
        def _():
            for b in range(G - 1):
                for which in range(2):
                    kv_wait(back, b, which)

    wait_early(0)

    nbm = tok // R
    zpart = z * nbm // n_head
    edge = n_head // 4
    outer = jnp.logical_or(z < edge, z >= n_head - edge)
    scale = HEAD ** -0.5 * math.log2(math.e)

    def where_of(s):
        blk = s // nch
        c = s % nch
        late = jnp.where(blk == 0, 0, jnp.where(blk == nblk - 1, 1, blk + 1))
        blk = jnp.where(outer, late, blk)
        b = G - 1 - blk % G
        part = (zpart + 1 + blk // G) % nbm
        return blk, c, b, part

    def out_copy(s, j):
        blk, c, b, part = where_of(s)
        dest = part * per_blk + j
        col = pl.multiple_of(z * (G * width) + a * width + c * cw, HEAD)
        src = obuf.at[s, pl.ds(j * T, T), :]
        dst = out_ref.at[:, pl.ds(col, cw)]
        idx = (z * G + a) * nch + c
        remote = pltpu.make_async_remote_copy(
            src_ref=src, dst_ref=dst, send_sem=osend.at[s * per_blk + j], recv_sem=orecv.at[idx],
            device_id=(k * G + b, dest), device_id_type=MESH)
        local = pltpu.make_async_copy(src, dst, orecv.at[idx])
        mine = jnp.logical_and(b == a, dest == z)
        return mine, remote, local

    def one_step(s, carry):
        blk, c, b, part = where_of(s)
        r0 = pl.multiple_of(b * tok + part * R, R)

        @pl.when(s == nch)
        def _():
            wait_late()

        @pl.when(c == 0)
        def _():
            rows = k * grp + r0 + lax.broadcasted_iota(jnp.int32, (R, HEAD), 0)
            start = starts_of(rows)
            for j in range(W // HEAD):
                t = (k - back) * grp + r0 + j * HEAD + lax.broadcasted_iota(jnp.int32, (R, HEAD), 1)
                ok = jnp.logical_and(t >= start, t <= rows)
                bias[:, j * HEAD:(j + 1) * HEAD] = jnp.where(ok, 0.0, -1e30)

        kcol = pl.ds(pl.multiple_of((c * chunk // per) * HEAD, HEAD), HEAD)
        keys = kvbuf[0, pl.ds(r0, W), kcol]
        q = qrot[pl.ds(c * chunk, chunk), pl.ds(r0, R), :].reshape(chunk * R, HEAD)
        sc = lax.dot_general(q, keys, (((1,), (1,)), ((), ())), preferred_element_type=jnp.float32)
        sc = (sc.reshape(chunk, R, W) + bias[...][None]).reshape(chunk * R, W)
        top = jnp.max(sc, axis=1, keepdims=True)
        w = jnp.exp2((sc - top) * scale).astype(jnp.bfloat16)

        @pl.when(s == 0)
        def _():
            wait_early(1)

        vals = kvbuf[1, pl.ds(r0, W), kcol]
        vals = jnp.concatenate([vals, jnp.ones_like(vals)], axis=1)
        acc = lax.dot_general(w, vals, (((1,), (0,)), ((), ())), preferred_element_type=jnp.float32)
        o = (acc[:, :HEAD] / acc[:, HEAD:]).astype(jnp.bfloat16)
        for h in range(chunk):
            obuf[s, :, h * HEAD:(h + 1) * HEAD] = o[h * R:(h + 1) * R, :]

        for j in range(per_blk):
            mine, remote, local = out_copy(s, j)

            @pl.when(mine)
            def _():
                local.start()

            @pl.when(jnp.logical_not(mine))
            def _():
                remote.start()
        return carry

    lax.fori_loop(0, nblk * nch, one_step, 0)

    for i in range(1, G):
        for which in (1, 0):
            kv_copy(0, i, which).wait_send()
    for c in q_copies:
        c.wait_send()
    for d in range(1, back + 1):
        @pl.when(sends(d))
        def _():
            for i in range(G):
                for which in (1, 0):
                    kv_copy(d, i, which).wait_send()
    if back >= 2:
        @pl.when(relays)
        def _():
            for which in range(2):
                relay_copy(G - 1, which).wait_send()

    def end_send(s, carry):
        for j in range(per_blk):
            mine, remote, local = out_copy(s, j)

            @pl.when(jnp.logical_not(mine))
            def _():
                remote.wait_send()
        return carry

    lax.fori_loop(0, nblk * nch, end_send, 0)

    def end_recv(i, carry):
        col = pl.multiple_of(i * cw, HEAD)
        ref = out_ref.at[:, pl.ds(col, cw)]
        pltpu.make_async_copy(ref, ref, orecv.at[i]).wait()
        return carry

    lax.fori_loop(0, n_head * G * nch, end_recv, 0)


def solution(mesh):
    n_srv, n_head = mesh.shape["srv"], mesh.shape["head"]

    def body(queries, key_value_pair, lengths):
        tok, qw = queries.shape
        kv_all = key_value_pair.shape[2] // HEAD
        G = 2 if kv_all % 2 == 0 and n_srv % 2 == 0 else 1
        kvh = kv_all // G
        per = qw // HEAD // kv_all
        grp = G * tok
        n_grp = n_srv // G
        back = n_grp // 2
        T = tok // n_head
        R = max(tok // 2, T)
        chunk = per // 2
        ndoc = lengths.shape[0]
        heads = kvh * per
        nsteps = (grp // R) * (heads // chunk)
        W = back * grp + R
        cfg = (n_srv, n_head, G, back, tok, kvh, per, R, chunk, ndoc)
        bf = jnp.bfloat16
        dma = pltpu.SemaphoreType.DMA
        return pl.pallas_call(
            functools.partial(kernel, cfg),
            out_shape=pltpu.VMEM((T, qw * n_head), bf),
            in_specs=[
                pl.BlockSpec(memory_space=pltpu.SMEM),
                pl.BlockSpec(memory_space=pl.ANY),
                pl.BlockSpec(memory_space=pl.ANY),
            ],
            out_specs=pl.BlockSpec(memory_space=pl.ANY),
            scratch_shapes=[
                pltpu.VMEM((G, tok, heads * HEAD), bf),
                pltpu.VMEM((heads, grp, HEAD), bf),
                pltpu.VMEM((2, (back + 1) * grp, kvh * HEAD), bf),
                pltpu.VMEM((2, tok, kv_all * HEAD), bf),
                pltpu.VMEM((tok, kv_all * HEAD), bf),
                pltpu.VMEM((2, tok, HEAD), jnp.float32),
                pltpu.VMEM((R, W), jnp.float32),
                pltpu.VMEM((nsteps, R, chunk * HEAD), bf),
                dma((2,)),
                dma((G,)),
                dma((G,)),
                dma((back + 1, G, 2)),
                dma((back + 1, G, 2)),
                dma((G, 2)),
                dma((nsteps * (R // T),)),
                dma((n_head * G * (heads // chunk),)),
            ],
            compiler_params=pltpu.CompilerParams(collective_id=0, has_side_effects=True),
            name="attend",
        )(lengths, queries, key_value_pair)

    in_specs = (P("srv", "head"), P(None, "srv", "head"), P())
    out_specs = P(("srv", "head"), None)
    return jax.shard_map(body, mesh=mesh, in_specs=in_specs, out_specs=out_specs, check_vma=False)
```

```python
import functools
import math

import jax
import jax.numpy as jnp
from jax import lax
from jax.experimental import pallas as pl
from jax.experimental.pallas import tpu as pltpu
from jax.sharding import PartitionSpec as P

HEAD = 128
MESH = pl.DeviceIdType.MESH


def kernel(cfg, len_ref, q_ref, kv_ref, out_ref, qraw, qrot, kvbuf, kvin, ksend, table, bias, obuf,
           lsem, qs, qr, kvs, kvr, fwd, osend, orecv):
    n_srv, n_head, G, back, tok, kvh, per, R, chunk, ndoc = cfg
    heads = kvh * per
    grp = G * tok
    n_grp = n_srv // G
    T = tok // n_head
    longest = back * grp
    W = longest + R
    width = heads * HEAD
    kw = kvh * HEAD
    nblk = grp // R
    nch = heads // chunk
    per_blk = R // T
    cw = chunk * HEAD
    srv = lax.axis_index("srv")
    z = lax.axis_index("head")
    k = srv // G
    a = srv % G

    bar = pltpu.get_barrier_semaphore()

    def greet(s, h):
        pl.semaphore_signal(bar, inc=1, device_id=(s, h), device_id_type=MESH)

    for i in range(1, n_head):
        for b in range(G):
            greet(k * G + b, (z + i) % n_head)
    for i in range(1, G):
        greet(k * G + (a + i) % G, z)
    for d in range(1, back + 1):
        @pl.when(k + d < n_grp)
        def _():
            for b in range(G):
                greet((k + d) * G + b, z)

        @pl.when(k - d >= 0)
        def _():
            for b in range(G):
                greet((k - d) * G + b, z)

    own_kv = pltpu.make_async_copy(kv_ref, kvin, lsem.at[0])
    own_kv.start()
    my_cols = pl.ds(pl.multiple_of(a * width, HEAD), width)
    own_q = pltpu.make_async_copy(q_ref.at[:, my_cols], qraw.at[a], lsem.at[1])
    own_q.start()

    for d in range(1, back + 1):
        @pl.when(k - d < 0)
        def _():
            kvbuf[:, pl.ds((back - d) * grp, grp), :] = jnp.zeros((2, grp, kw), jnp.bfloat16)

    ends = []
    total = jnp.int32(0)
    for i in range(ndoc):
        total = total + len_ref[i]
        ends.append(total)

    lane = lax.broadcasted_iota(jnp.int32, (tok, HEAD), 1)
    low = lane < HEAD // 2
    step_up = jnp.where(low, lane, lane - HEAD // 2).astype(jnp.float32) * (2.0 / HEAD)
    inverse = jnp.exp(-step_up * math.log(500000.0))

    def starts_of(rows):
        start = jnp.zeros_like(rows)
        for e in ends:
            start = jnp.where(e <= rows, e, start)
        return start

    def make_table(b):
        rows = (k * G + b) * tok + lax.broadcasted_iota(jnp.int32, (tok, HEAD), 0)
        angle = (rows - starts_of(rows)).astype(jnp.float32) * inverse
        sine = jnp.sin(angle)
        table[0] = jnp.cos(angle)
        table[1] = jnp.where(low, -sine, sine)

    def rotate(x):
        x = x.astype(jnp.float32)
        return (x * table[0] + pltpu.roll(x, HEAD // 2, 1) * table[1]).astype(jnp.bfloat16)

    make_table(a)
    own_kv.wait()
    for h in range(G * kvh):
        cols = slice(h * HEAD, (h + 1) * HEAD)
        ksend[:, cols] = rotate(kvin[0, :, cols])

    own_rows = pl.ds(pl.multiple_of(back * grp + a * tok, tok), tok)
    kv_cols = pl.ds(pl.multiple_of(a * kw, HEAD), kw)
    kvbuf[0, own_rows, :] = ksend[:, kv_cols]
    kvbuf[1, own_rows, :] = kvin[1, :, kv_cols]

    count = (n_head - 1) * G + (G - 1)
    for d in range(1, back + 1):
        count = count + G * jnp.where(k + d < n_grp, 1, 0) + G * jnp.where(k - d >= 0, 1, 0)
    pl.semaphore_wait(bar, count)

    def kv_copy(d, i, which):
        b = (a + i) % G
        cols = pl.ds(pl.multiple_of(b * kw, HEAD), kw)
        src = ksend.at[:, cols] if which == 0 else kvin.at[1, :, cols]
        rows = pl.ds(pl.multiple_of((back - d) * grp + a * tok, tok), tok)
        return pltpu.make_async_remote_copy(
            src_ref=src, dst_ref=kvbuf.at[which, rows, :],
            send_sem=kvs.at[d, i, which], recv_sem=kvr.at[d, a, which],
            device_id=((k + d) * G + b, z), device_id_type=MESH)

    def kv_wait(d, b, which):
        rows = pl.ds(pl.multiple_of((back - d) * grp + b * tok, tok), tok)
        ref = kvbuf.at[which, rows, :]
        pltpu.make_async_copy(ref, ref, kvr.at[d, b, which]).wait()

    relayed = jnp.logical_and(jnp.logical_and(k % 2 == 1, k + 2 < n_grp), a == G - 1)
    relays = jnp.logical_and(k % 2 == 1, k >= 3)

    def sends(d):
        near = k + d < n_grp
        if d == 1 and back >= 2:
            near = jnp.logical_and(near, jnp.logical_not(relayed))
        return near

    def relay_copy(b, which):
        src = pl.ds(pl.multiple_of((back - 2) * grp + b * tok, tok), tok)
        dst = pl.ds(pl.multiple_of((back - 1) * grp + b * tok, tok), tok)
        return pltpu.make_async_remote_copy(
            src_ref=kvbuf.at[which, src, :], dst_ref=kvbuf.at[which, dst, :],
            send_sem=fwd.at[b, which], recv_sem=kvr.at[1, b, which],
            device_id=(srv - G, z), device_id_type=MESH)

    def start_kv(d, when):
        @pl.when(jnp.logical_and(sends(d), when))
        def _():
            pairs = [(i, which) for which in range(2) for i in range(G)]
            for i, which in pairs if d == 1 else sorted(pairs):
                kv_copy(d, i, which).start()

    for d in range(1, back + 1):
        start_kv(d, a == G - 1 if d == back else True)
    q_copies = []
    for i in range(1, G):
        b = (a + i) % G
        for which in range(2):
            kv_copy(0, i, which).start()
        cols = pl.ds(pl.multiple_of(b * width, HEAD), width)
        c = pltpu.make_async_remote_copy(
            src_ref=q_ref.at[:, cols], dst_ref=qraw.at[a],
            send_sem=qs.at[i], recv_sem=qr.at[a],
            device_id=(k * G + b, z), device_id_type=MESH)
        c.start()
        q_copies.append(c)

    def rotate_queries(b):
        for h in range(heads):
            qrot[h, pl.ds(pl.multiple_of(b * tok, tok), tok), :] = rotate(
                qraw[b, :, h * HEAD:(h + 1) * HEAD])

    own_q.wait()
    rotate_queries(a)
    start_kv(back, a < G - 1)
    for i in range(1, G):
        b = (a + i) % G
        make_table(b)
        pltpu.make_async_copy(qraw.at[b], qraw.at[b], qr.at[b]).wait()
        rotate_queries(b)

    if back >= 2:
        @pl.when(k >= 2)
        def _():
            kv_wait(2, G - 1, 0)

            @pl.when(relays)
            def _():
                relay_copy(G - 1, 0).start()
                kv_wait(2, G - 1, 1)
                relay_copy(G - 1, 1).start()

    def wait_early(which):
        for i in range(1, G):
            kv_wait(0, (a + i) % G, which)
        if which == 1 and back >= 2:
            @pl.when(jnp.logical_and(k >= 2, jnp.logical_not(relays)))
            def _():
                kv_wait(2, G - 1, 1)
        for d in range(1, back + 1):
            @pl.when(k - d >= 0)
            def _():
                for b in range(G - 1 if d == back else 0, G):
                    if (d, b) != (2, G - 1):
                        kv_wait(d, b, which)

    def wait_late():
        @pl.when(k - back >= 0)
        def _():
            for b in range(G - 1):
                for which in range(2):
                    kv_wait(back, b, which)

    wait_early(0)

    nbm = tok // R
    zpart = z * nbm // n_head
    edge = n_head // 4
    outer = jnp.logical_or(z < edge, z >= n_head - edge)
    scale = HEAD ** -0.5 * math.log2(math.e)

    def where_of(s):
        blk = s // nch
        c = s % nch
        late = jnp.where(blk == 0, 0, jnp.where(blk == nblk - 1, 1, blk + 1))
        blk = jnp.where(outer, late, blk)
        b = G - 1 - blk % G
        part = (zpart + 1 + blk // G) % nbm
        return blk, c, b, part

    def out_copy(s, j):
        blk, c, b, part = where_of(s)
        dest = part * per_blk + j
        col = pl.multiple_of(z * (G * width) + a * width + c * cw, HEAD)
        src = obuf.at[s, pl.ds(j * T, T), :]
        dst = out_ref.at[:, pl.ds(col, cw)]
        idx = (z * G + a) * nch + c
        remote = pltpu.make_async_remote_copy(
            src_ref=src, dst_ref=dst, send_sem=osend.at[s * per_blk + j], recv_sem=orecv.at[idx],
            device_id=(k * G + b, dest), device_id_type=MESH)
        local = pltpu.make_async_copy(src, dst, orecv.at[idx])
        mine = jnp.logical_and(b == a, dest == z)
        return mine, remote, local

    def one_step(s, carry):
        blk, c, b, part = where_of(s)
        r0 = pl.multiple_of(b * tok + part * R, R)

        @pl.when(s == nch)
        def _():
            wait_late()

        @pl.when(c == 0)
        def _():
            rows = k * grp + r0 + lax.broadcasted_iota(jnp.int32, (R, HEAD), 0)
            start = starts_of(rows)
            for j in range(W // HEAD):
                t = (k - back) * grp + r0 + j * HEAD + lax.broadcasted_iota(jnp.int32, (R, HEAD), 1)
                ok = jnp.logical_and(t >= start, t <= rows)
                bias[:, j * HEAD:(j + 1) * HEAD] = jnp.where(ok, 0.0, -1e30)

        kcol = pl.ds(pl.multiple_of((c * chunk // per) * HEAD, HEAD), HEAD)
        keys = kvbuf[0, pl.ds(r0, W), kcol]
        q = qrot[pl.ds(c * chunk, chunk), pl.ds(r0, R), :].reshape(chunk * R, HEAD)
        sc = lax.dot_general(q, keys, (((1,), (1,)), ((), ())), preferred_element_type=jnp.float32)
        sc = (sc.reshape(chunk, R, W) + bias[...][None]).reshape(chunk * R, W)
        top = jnp.max(sc, axis=1, keepdims=True)
        w = jnp.exp2((sc - top) * scale).astype(jnp.bfloat16)

        @pl.when(s == 0)
        def _():
            wait_early(1)

        vals = kvbuf[1, pl.ds(r0, W), kcol]
        vals = jnp.concatenate([vals, jnp.ones_like(vals)], axis=1)
        acc = lax.dot_general(w, vals, (((1,), (0,)), ((), ())), preferred_element_type=jnp.float32)
        o = (acc[:, :HEAD] / acc[:, HEAD:]).astype(jnp.bfloat16)
        for h in range(chunk):
            obuf[s, :, h * HEAD:(h + 1) * HEAD] = o[h * R:(h + 1) * R, :]

        for j in range(per_blk):
            mine, remote, local = out_copy(s, j)

            @pl.when(mine)
            def _():
                local.start()

            @pl.when(jnp.logical_not(mine))
            def _():
                remote.start()
        return carry

    lax.fori_loop(0, nblk * nch, one_step, 0)

    for i in range(1, G):
        for which in (1, 0):
            kv_copy(0, i, which).wait_send()
    for c in q_copies:
        c.wait_send()
    for d in range(1, back + 1):
        @pl.when(sends(d))
        def _():
            for i in range(G):
                for which in (1, 0):
                    kv_copy(d, i, which).wait_send()
    if back >= 2:
        @pl.when(relays)
        def _():
            for which in range(2):
                relay_copy(G - 1, which).wait_send()

    def end_send(s, carry):
        for j in range(per_blk):
            mine, remote, local = out_copy(s, j)

            @pl.when(jnp.logical_not(mine))
            def _():
                remote.wait_send()
        return carry

    lax.fori_loop(0, nblk * nch, end_send, 0)

    def end_recv(i, carry):
        col = pl.multiple_of(i * cw, HEAD)
        ref = out_ref.at[:, pl.ds(col, cw)]
        pltpu.make_async_copy(ref, ref, orecv.at[i]).wait()
        return carry

    lax.fori_loop(0, n_head * G * nch, end_recv, 0)


def solution(mesh):
    n_srv, n_head = mesh.shape["srv"], mesh.shape["head"]

    def body(queries, key_value_pair, lengths):
        tok, qw = queries.shape
        kv_all = key_value_pair.shape[2] // HEAD
        G = 2 if kv_all % 2 == 0 and n_srv % 2 == 0 else 1
        kvh = kv_all // G
        per = qw // HEAD // kv_all
        grp = G * tok
        n_grp = n_srv // G
        back = n_grp // 2
        T = tok // n_head
        R = max(tok // 2, T)
        chunk = per // 2
        ndoc = lengths.shape[0]
        heads = kvh * per
        nsteps = (grp // R) * (heads // chunk)
        W = back * grp + R
        cfg = (n_srv, n_head, G, back, tok, kvh, per, R, chunk, ndoc)
        bf = jnp.bfloat16
        dma = pltpu.SemaphoreType.DMA
        return pl.pallas_call(
            functools.partial(kernel, cfg),
            out_shape=pltpu.VMEM((T, qw * n_head), bf),
            in_specs=[
                pl.BlockSpec(memory_space=pltpu.SMEM),
                pl.BlockSpec(memory_space=pl.ANY),
                pl.BlockSpec(memory_space=pl.ANY),
            ],
            out_specs=pl.BlockSpec(memory_space=pl.ANY),
            scratch_shapes=[
                pltpu.VMEM((G, tok, heads * HEAD), bf),
                pltpu.VMEM((heads, grp, HEAD), bf),
                pltpu.VMEM((2, (back + 1) * grp, kvh * HEAD), bf),
                pltpu.VMEM((2, tok, kv_all * HEAD), bf),
                pltpu.VMEM((tok, kv_all * HEAD), bf),
                pltpu.VMEM((2, tok, HEAD), jnp.float32),
                pltpu.VMEM((R, W), jnp.float32),
                pltpu.VMEM((nsteps, R, chunk * HEAD), bf),
                dma((2,)),
                dma((G,)),
                dma((G,)),
                dma((back + 1, G, 2)),
                dma((back + 1, G, 2)),
                dma((G, 2)),
                dma((nsteps * (R // T),)),
                dma((n_head * G * (heads // chunk),)),
            ],
            compiler_params=pltpu.CompilerParams(collective_id=0, has_side_effects=True),
            name="attend",
        )(lengths, queries, key_value_pair)

    in_specs = (P("srv", "head"), P(None, "srv", "head"), P())
    out_specs = P(("srv", "head"), None)
    return jax.shard_map(body, mesh=mesh, in_specs=in_specs, out_specs=out_specs, check_vma=False)
```
